32 devices in a mesh: seq: 16 (over z, x, core), tp: 2 (over y).
Axes of the slice: x: 2, y: 2, z: 4, core: 2. Of those that a mesh axis runs over, the one named last changes fastest.
Arguments:
- tokens: bfloat16 [8192, 1024], P(('seq', 'tp')), may hold values from -6 to 6
- w_query: bfloat16 [2, 1024, 1024], replicated, may hold values from -0.1875 to 0.1875
- w_key: bfloat16 [2, 1024, 1024], replicated, may hold values from -0.1875 to 0.1875
- w_value: bfloat16 [2, 1024, 1024], replicated, may hold values from -0.1875 to 0.1875
- w_gate: bfloat16 [2, 1024, 1024], replicated, may hold values from -0.1875 to 0.1875
- w_out: bfloat16 [2, 1024, 1024], replicated, may hold values from -0.1875 to 0.1875
- w_first: bfloat16 [2, 1024, 2816], P(None, None, 'tp'), may hold values from -0.1875 to 0.1875
- w_second: bfloat16 [2, 1024, 2816], P(None, None, 'tp'), may hold values from -0.1875 to 0.1875
- w_third: bfloat16 [2, 2816, 1024], P(None, 'tp'), may hold values from -0.109375 to 0.109375
- decay: float32 [8], replicated, may hold values from 1e-05 to 0.04
- doc_lengths: int32 [3], replicated, may hold values from 1 to 4, as said below
- cotangent: bfloat16 [8192, 1024], P(('seq', 'tp')), may hold values from -6 to 6
Outputs:
- mixed: bfloat16 [8192, 1024], P(('seq', 'tp'))
- token_grad: float32 [8192, 1024], P(('seq', 'tp'))
- grad_query: float32 [2, 1024, 1024], P(None, ('seq', 'tp'))
- grad_key: float32 [2, 1024, 1024], P(None, ('seq', 'tp'))
- grad_value: float32 [2, 1024, 1024], P(None, ('seq', 'tp'))
- grad_gate: float32 [2, 1024, 1024], P(None, ('seq', 'tp'))
- grad_out: float32 [2, 1024, 1024], P(None, ('seq', 'tp'))
- grad_first: float32 [2, 1024, 2816], P(None, 'seq', 'tp')
- grad_second: float32 [2, 1024, 2816], P(None, 'seq', 'tp')
- grad_third: float32 [2, 2816, 1024], P(None, 'tp', 'seq')
The draws below stay inside these ranges and needn't reach their ends.
Inputs may be any that keep to these rules, and one draw needn't show every extreme that they name: `doc_lengths`: the lengths sum to 8.
All inputs are finite; a program needn't handle non-finite values.
Results may differ from the reference program's by a relative error of at most 0.024.
Values may be sent and summed in bfloat16 or wider, within the bound.
No kernel may reach another device: no remote copies, remote signals or barrier semaphores. Data moves between devices by JAX's collectives and lax.ppermute only.
A program may use at most 576 MiB of HBM per device.

```python
import math
import jax
import jax.numpy as jnp
from jax import lax

D = 1024
H = 8
FF = 2816
LAYERS = 2
BLOCK = 256
UNIT = 1024
TOKENS = 8192
UNITS = 8
LONGEST = 4
DOCS = 3


def split_units(key, total, count):
    pieces = []
    left_over = total - count
    for number in range(count):
        remaining = count - 1 - number
        lowest = jnp.maximum(0, left_over - remaining * (LONGEST - 1))
        highest = jnp.minimum(LONGEST - 1, left_over)
        extra = jax.random.randint(jax.random.fold_in(key, number), (), lowest, highest + 1, dtype=jnp.int32)
        pieces.append(1 + extra)
        left_over = left_over - extra
    return pieces


def draw_doc_lengths(key, part):
    before = (DOCS - 1) // 2
    after = DOCS - 1 - before
    lowest = max(max(before, UNITS // 2 - LONGEST + 2), UNITS - LONGEST - after * LONGEST)
    highest = min(min(before * LONGEST, UNITS // 2 - 1), UNITS - LONGEST - after)
    prefix = jax.random.randint(jax.random.fold_in(key, 7), (), lowest, highest + 1, dtype=jnp.int32)
    suffix = UNITS - LONGEST - prefix
    front = split_units(jax.random.fold_in(key, 11), prefix, before)
    back = split_units(jax.random.fold_in(key, 13), suffix, after)
    pieces = front + [jnp.full((), LONGEST, jnp.int32)] + back
    return jnp.stack(pieces).astype(jnp.int32)


def levels(stream_key, extent, shards, smallest, top_value):
    loudness, own = 1.0, jax.random.fold_in(stream_key, 6)
    for axis_at, parts in shards:
        draws = jnp.exp(jax.random.uniform(jax.random.fold_in(own, axis_at), (parts,), jnp.float32, smallest / len(shards), top_value / len(shards)))
        loudness = loudness * jnp.repeat(draws, extent[axis_at] // parts).reshape([-1 if axis == axis_at else 1 for axis in range(len(extent))])
    return loudness


def normal_values(key, dims, width, bound, split=(), held_as=jnp.bfloat16):
    gain = levels(key, dims, split, -0.22, 0.18) if split else 1.0
    array = jax.random.normal(key, dims, jnp.float32) * width * gain
    return jnp.minimum(jnp.maximum(array, -bound), bound).astype(held_as)


def setup_inputs(seed: int = 0) -> dict:
    keys = jax.random.split(jax.random.key(seed), 13)
    tokens = normal_values(keys[0], (TOKENS, D), 1.0, 6.0, ((0, 32),))
    w_query = normal_values(keys[1], (LAYERS, D, D), D ** -0.5, 0.1875)
    w_key = normal_values(keys[2], (LAYERS, D, D), D ** -0.5, 0.1875)
    w_value = normal_values(keys[3], (LAYERS, D, D), D ** -0.5, 0.1875)
    w_gate = normal_values(keys[4], (LAYERS, D, D), D ** -0.5, 0.1875)
    w_out = normal_values(keys[5], (LAYERS, D, D), D ** -0.5, 0.1875)
    w_first = normal_values(keys[6], (LAYERS, D, FF), D ** -0.5, 0.1875, ((2, 2),))
    w_second = normal_values(keys[7], (LAYERS, D, FF), D ** -0.5, 0.1875, ((2, 2),))
    w_third = normal_values(keys[8], (LAYERS, FF, D), FF ** -0.5, 0.109375, ((1, 2),))
    decay = jnp.clip(jnp.exp(jax.random.uniform(keys[9], (H,), jnp.float32, math.log(9.999999747378752e-06), math.log(0.04))), 9.999999747378752e-06, 0.04)
    doc_lengths = draw_doc_lengths(jax.random.fold_in(keys[12], 71), 0)
    cotangent = normal_values(keys[11], (TOKENS, D), 1.0, 6.0, ((0, 32),))
    return dict(tokens=tokens, w_query=w_query, w_key=w_key, w_value=w_value, w_gate=w_gate, w_out=w_out, w_first=w_first, w_second=w_second, w_third=w_third, decay=decay, doc_lengths=doc_lengths, cotangent=cotangent)


EPS = 1e-06
HIGHEST = lax.Precision.HIGHEST

@jax.custom_vjp
def low(v):
    return lax.optimization_barrier(v.astype(jnp.bfloat16)).astype(jnp.float32)

@jax.custom_vjp
def low_back(v):
    return v

def low_keep(v):
    return (low(v), None)

def low_pass(kept, grad):
    return (grad,)

def back_keep(v):
    return (v, None)

def back_low(kept, grad):
    return (low(grad),)
low.defvjp(low_keep, low_pass)
low_back.defvjp(back_keep, back_low)

def inverse_rms(values):
    return lax.rsqrt(lax.optimization_barrier(jnp.mean(values * values, axis=-1, keepdims=True)) + EPS)

def rotary_tables(positions, columns):
    shifts = jnp.arange(columns, dtype=jnp.int32) * 13 // columns
    speeds = jnp.right_shift(jnp.full((columns,), 8192, jnp.int32), shifts)
    phases = positions[:, None] % 65536 * speeds[None, :] % 65536
    angles = phases.astype(jnp.float32) * (2.0 * math.pi / 65536.0)
    return (jnp.cos(angles), jnp.sin(angles))

def decay_tables(rates, length):
    spots = jnp.arange(length, dtype=jnp.float32)
    gaps = spots[:, None] - spots[None, :]
    mask = jnp.where(gaps[None] >= 0, jnp.exp(-rates[:, None, None] * jnp.maximum(gaps, 0.0)[None]), 0.0)
    inward = jnp.exp(-rates[None, :] * (spots[:, None] + 1.0))
    outward = jnp.exp(-rates[None, :] * (length - 1.0 - spots[:, None]))
    return (mask, inward, outward, jnp.exp(-rates * length))

def matmul(left, right):
    return jnp.dot(left, right, precision=HIGHEST, preferred_element_type=jnp.float32)

def rotate(acts, cosine_table, sine_table, heads):
    row_count, model_width = acts.shape
    shaped = acts.reshape(row_count, heads, model_width // heads)
    return jnp.concatenate([shaped * cosine_table[:, None, :], shaped * sine_table[:, None, :]], axis=-1)

def lightning(query_rot, key_rot, values, flags, tables):
    mask, inward, outward, whole = tables
    row_count, heads, double = query_rot.shape
    head_size = values.shape[2]
    block_count = row_count // BLOCK

    def step(state, inputs):
        query, key, value, start = inputs
        state = state * (1.0 - start)
        raw = jnp.einsum('ihe,jhe->hij', query, key, precision=HIGHEST)
        weights = low(low_back(raw) * mask)
        intra = jnp.einsum('hij,jhf->ihf', weights, value, precision=HIGHEST)
        query_scaled = low(query * inward[:, :, None])
        inter = jnp.einsum('ihe,hef->ihf', query_scaled, low(state), precision=HIGHEST)
        key_scaled = low(key * outward[:, :, None])
        contrib = low_back(jnp.einsum('jhe,jhf->hef', key_scaled, value, precision=HIGHEST))
        return (whole[:, None, None] * state + contrib, intra + inter)
    initial = jnp.zeros((heads, double, head_size), jnp.float32)
    inputs = (query_rot.reshape(block_count, BLOCK, heads, double), key_rot.reshape(block_count, BLOCK, heads, double), values.reshape(block_count, BLOCK, heads, head_size), flags)
    _, outputs = lax.scan(jax.checkpoint(step), initial, inputs)
    return outputs.reshape(row_count, heads * head_size)

def reference(tokens, w_query, w_key, w_value, w_gate, w_out, w_first, w_second, w_third, decay, doc_lengths, cotangent):
    row_count, model_width = tokens.shape
    heads = decay.shape[0]
    head_size = model_width // heads
    block_count = row_count // BLOCK
    ends = jnp.cumsum(doc_lengths, dtype=jnp.int32) * UNIT
    starts = jnp.concatenate([jnp.zeros((1,), jnp.int32), ends[:-1].astype(jnp.int32)])
    block_first = jnp.arange(block_count, dtype=jnp.int32) * BLOCK
    flags = jnp.any(block_first[:, None] == starts[None, :], axis=1).astype(jnp.float32)
    positions = jnp.arange(row_count, dtype=jnp.int32)
    cosine_table, sine_table = rotary_tables(positions, head_size)
    tables = decay_tables(decay.astype(jnp.float32), BLOCK)

    def forward(stream, wq, wk, wv, wu, wo, wone, wtwo, wthree):
        for layer_index in range(LAYERS):
            normed_one = low(stream * inverse_rms(stream))
            query_pre = low_back(matmul(normed_one, wq[layer_index]))
            key_pre = low_back(matmul(normed_one, wk[layer_index]))
            value_low = low(low_back(matmul(normed_one, wv[layer_index])))
            gate_pre = low_back(matmul(normed_one, wu[layer_index]))
            query_rot = low(rotate(jax.nn.silu(query_pre), cosine_table, sine_table, heads))
            key_rot = low(rotate(jax.nn.silu(key_pre), cosine_table, sine_table, heads))
            attended = low_back(lightning(query_rot, key_rot, value_low.reshape(row_count, heads, head_size), flags, tables))
            mixed_heads = low(attended * inverse_rms(attended) * gate_pre)
            hidden = stream + low_back(matmul(mixed_heads, wo[layer_index]))
            normed_two = low(hidden * inverse_rms(hidden))
            first_act = low_back(matmul(normed_two, wone[layer_index]))
            second_act = low_back(matmul(normed_two, wtwo[layer_index]))
            product = low(first_act * second_act)
            stream = hidden + low_back(matmul(product, wthree[layer_index]))
        return stream
    result, pullback = jax.vjp(forward, tokens.astype(jnp.float32), w_query.astype(jnp.float32), w_key.astype(jnp.float32), w_value.astype(jnp.float32), w_gate.astype(jnp.float32), w_out.astype(jnp.float32), w_first.astype(jnp.float32), w_second.astype(jnp.float32), w_third.astype(jnp.float32))
    grads = pullback(cotangent.astype(jnp.float32))
    return (result.astype(jnp.bfloat16), grads[0], grads[1], grads[2], grads[3], grads[4], grads[5], grads[6], grads[7], grads[8])
```

```python
import math

import jax
import jax.numpy as jnp
from jax import lax
from jax.sharding import PartitionSpec as P

BLOCK = 256
UNIT = 1024


EPS = 1e-06


AXES = ("seq", "tp")
TP_BIT, CORE_BIT, X_BIT, OUTER_BIT = 1, 2, 4, 8


def device_count():
    return lax.axis_size("seq") * lax.axis_size("tp")


def device_index():
    return lax.axis_index("seq") * lax.axis_size("tp") + lax.axis_index("tp")


def swap(value, flip):
    return lax.ppermute(value, AXES, [(i, i ^ flip) for i in range(device_count())])


def shift(value, distance):
    count = device_count()
    pairs = [(i, i + distance) for i in range(count) if 0 <= i + distance < count]
    return lax.ppermute(value, AXES, pairs)


def low(value):
    return value.astype(jnp.bfloat16)


def wide(value):
    return value.astype(jnp.float32)


def inverse_rms(values):
    return lax.rsqrt(jnp.mean(values * values, axis=-1, keepdims=True) + EPS)


def rms_back(values, scale, grads):
    return scale * grads - values * (scale * scale * scale) * jnp.mean(
        grads * values, axis=-1, keepdims=True
    )


def rotary_tables(positions, columns):
    shifts = jnp.arange(columns, dtype=jnp.int32) * 13 // columns
    speeds = jnp.right_shift(jnp.full((columns,), 8192, jnp.int32), shifts)
    phases = positions[:, None] % 65536 * speeds[None, :] % 65536
    angles = phases.astype(jnp.float32) * (2.0 * math.pi / 65536.0)
    return (jnp.cos(angles), jnp.sin(angles))


def decay_tables(rates, length):
    spots = jnp.arange(length, dtype=jnp.float32)
    gaps = spots[:, None] - spots[None, :]
    mask = jnp.where(
        gaps[None] >= 0, jnp.exp(-rates[:, None, None] * jnp.maximum(gaps, 0.0)[None]), 0.0
    )
    inward = jnp.exp(-rates[None, :] * (spots[:, None] + 1.0))
    outward = jnp.exp(-rates[None, :] * (length - 1.0 - spots[:, None]))
    return (mask, inward, outward, jnp.exp(-rates * length))


def rotate(acts, cosine_table, sine_table, heads):
    row_count, model_width = acts.shape
    shaped = acts.reshape(row_count, heads, model_width // heads)
    return jnp.concatenate(
        [shaped * cosine_table[:, None, :], shaped * sine_table[:, None, :]], axis=-1
    )


def unrotate(grads, cosine_table, sine_table):
    half = grads.shape[-1] // 2
    plain = (
        grads[..., :half] * cosine_table[:, None, :] + grads[..., half:] * sine_table[:, None, :]
    )
    return plain.reshape(grads.shape[0], -1)


def swish_slope(values):
    logistic = jax.nn.sigmoid(values)
    return logistic * (1.0 + values * (1.0 - logistic))


def contract_rows(left, right):
    return lax.dot_general(
        left, right, (((0,), (0,)), ((), ())), preferred_element_type=jnp.float32
    )


def contract_cols(left, right):
    return lax.dot_general(
        left, right, (((1,), (1,)), ((), ())), preferred_element_type=jnp.float32
    )


def owner_order(rows, bits):
    count = 1 << len(bits)
    size = rows // count
    order = []
    for number in range(count):
        owner = 0
        for place, bit in enumerate(reversed(bits)):
            owner |= ((number >> place) & 1) * bit
        order.append(owner)
    relative = jnp.repeat(jnp.asarray(order, jnp.int32), size)
    return relative, size


def owner_select(rows, bits, drop):
    relative, size = owner_order(rows, bits)
    chosen = ((relative ^ device_index()) >> drop) * size + jnp.arange(rows, dtype=jnp.int32) % size
    return (jnp.arange(rows, dtype=jnp.int32)[:, None] == chosen[None, :]).astype(jnp.bfloat16)


def outer_bits():
    bits, bit = [], device_count() // 2
    while bit >= OUTER_BIT:
        bits.append(bit)
        bit //= 2
    return bits


def sum_outer(block, size):
    total = wide(block[:size])
    for number in range(1, block.shape[0] // size):
        total = total + wide(swap(block[number * size : (number + 1) * size], number * OUTER_BIT))
    return total


def reduce_weight(left, right, tail):
    rows = left.shape[1]
    half, quarter = rows // 2, rows // 4
    from_core = swap(low(contract_rows(left[:, half:], right)), CORE_BIT)
    away = low(contract_rows(left[:, quarter:half], right) + wide(from_core[quarter:]))
    from_x = swap(away, X_BIT)
    mine = contract_rows(left[:, :quarter], right) + wide(from_core[:quarter]) + wide(from_x)
    outer = device_count() // OUTER_BIT
    mine = low(mine)
    if tail == "none":
        return sum_outer(mine, quarter // outer)
    if tail == "outer_tp":
        mine = low(sum_outer(mine, quarter // outer))
        size = mine.shape[0] // 2
        return wide(mine[:size]) + wide(swap(mine[size:], TP_BIT))
    size = mine.shape[0] // 2
    mine = low(wide(mine[:size]) + wide(swap(mine[size:], TP_BIT)))
    return sum_outer(mine, size // outer)


def pair_powers(decay, exponent):
    exponent = exponent.astype(jnp.float32)
    return jnp.where(exponent >= 0, jnp.exp(-decay * BLOCK * jnp.maximum(exponent, 0.0)), 0.0)


def state_exchange(contrib, decay, doc_lengths, backward):
    heads, wide_size, head_size = contrib.shape
    members = UNIT // BLOCK
    device = device_index()
    member = device % members
    unit = device // members
    units = device_count() // members
    part = heads // members
    longest = units // 2
    parts = low(contrib).reshape(members, part, wide_size, head_size)

    def part_of(array, index):
        return lax.dynamic_index_in_dim(array, index, 0, keepdims=False)

    mine = [part_of(parts, member)]
    for flip in range(1, members):
        mine.append(swap(part_of(parts, member ^ flip), flip))
    rates = part_of(decay.reshape(members, part), member)

    def place(flip):
        number = member ^ flip
        return members - 1 - number if backward else number

    def scaled(power, value):
        return power[:, None, None] * wide(value)

    total = sum(scaled(pair_powers(rates, members - 1 - place(flip)), mine[flip]) for flip in range(members))
    ends = jnp.cumsum(doc_lengths, dtype=jnp.int32)
    starts = jnp.concatenate([jnp.zeros((1,), jnp.int32), ends[:-1]])

    def joined(number):
        first = number + 1 if backward else number
        inside = (first > 0) & (first < units)
        return jnp.where(inside & ~jnp.any(first == starts), 1.0, 0.0)

    direction = -1 if backward else 1
    window = total
    entering = jnp.zeros_like(total)
    distance = 1
    links = joined(unit)
    while distance < longest:
        received = shift(low(window), direction * distance * members)
        entering = entering + scaled(links * pair_powers(rates, jnp.int32(members * (distance - 1))), received)
        if 2 * distance < longest:
            window = window + scaled(links * pair_powers(rates, jnp.int32(members * distance)), received)
            for step in range(distance, 2 * distance):
                links = links * joined(unit - direction * step)
        distance *= 2
    results = []
    for flip in range(members):
        target = place(flip)
        value = scaled(pair_powers(rates, target), entering)
        for source in range(members):
            value = value + scaled(pair_powers(rates, target - 1 - place(source)), mine[source])
        value = low(value)
        results.append(swap(value, flip) if flip else value)
    stacked = jnp.stack(results)
    back = jnp.stack([part_of(stacked, member ^ number) for number in range(members)])
    return back.reshape(heads, wide_size, head_size)


def local(
    tokens,
    w_query,
    w_key,
    w_value,
    w_gate,
    w_out,
    w_first,
    w_second,
    w_third,
    decay,
    doc_lengths,
    cotangent,
):
    length, model_width = tokens.shape
    heads = decay.shape[0]
    head_size = model_width // heads
    double = 2 * head_size
    layer_count = w_query.shape[0]
    positions = device_index() * length + jnp.arange(length, dtype=jnp.int32)
    cosine_table, sine_table = rotary_tables(positions, head_size)
    mask, inward, outward, _ = decay_tables(decay, BLOCK)
    inward_wide = inward[:, :, None]
    outward_wide = outward[:, :, None]
    attention_select = owner_select(model_width, [CORE_BIT, X_BIT, *outer_bits(), TP_BIT], 0)
    attention_select_last = owner_select(model_width, [CORE_BIT, X_BIT, TP_BIT, *outer_bits()], 0)
    ffn_select = owner_select(model_width, [CORE_BIT, X_BIT, *outer_bits()], 1)

    def chosen(array, select):
        return low(jnp.dot(array, select, preferred_element_type=jnp.float32))

    stream = tokens.astype(jnp.float32)
    saved = []
    for layer_index in range(layer_count):
        first_scale = inverse_rms(stream)
        normed_one = low(stream * first_scale)
        key_pre = jnp.dot(normed_one, w_key[layer_index], preferred_element_type=jnp.float32)
        value_pre = jnp.dot(normed_one, w_value[layer_index], preferred_element_type=jnp.float32)
        key_rot = low(rotate(jax.nn.silu(key_pre), cosine_table, sine_table, heads))
        values = low(value_pre).reshape(length, heads, head_size)
        key_scaled = low(key_rot * outward_wide)
        contrib = jnp.einsum("jhe,jhf->hef", key_scaled, values, preferred_element_type=jnp.float32)
        states = state_exchange(contrib, decay, doc_lengths, False)
        query_pre = jnp.dot(normed_one, w_query[layer_index], preferred_element_type=jnp.float32)
        gate_pre = jnp.dot(normed_one, w_gate[layer_index], preferred_element_type=jnp.float32)
        query_rot = low(rotate(jax.nn.silu(query_pre), cosine_table, sine_table, heads))
        raw = jnp.einsum("ihe,jhe->hij", query_rot, key_rot, preferred_element_type=jnp.float32)
        weights = low(raw * mask)
        intra = jnp.einsum("hij,jhf->ihf", weights, values, preferred_element_type=jnp.float32)
        query_scaled = low(query_rot * inward_wide)
        inter = jnp.einsum("ihe,hef->ihf", query_scaled, states, preferred_element_type=jnp.float32)
        attended = (intra + inter).reshape(length, model_width)
        out_scale = inverse_rms(attended)
        normed_out = attended * out_scale
        mixed_heads = low(normed_out * gate_pre)
        hidden = stream + jnp.dot(mixed_heads, w_out[layer_index], preferred_element_type=jnp.float32)
        second_scale = inverse_rms(hidden)
        normed_two = low(hidden * second_scale)
        normed_other = swap(normed_two, TP_BIT)

        def ffn(normed):
            first_act = jnp.dot(normed, w_first[layer_index], preferred_element_type=jnp.float32)
            second_act = jnp.dot(normed, w_second[layer_index], preferred_element_type=jnp.float32)
            product = low(first_act * second_act)
            out = jnp.dot(product, w_third[layer_index], preferred_element_type=jnp.float32)
            return first_act, second_act, product, out

        other = ffn(normed_other)
        own = ffn(normed_two)
        glu_out = own[3] + wide(swap(low(other[3]), TP_BIT))
        saved.append(
            (
                stream,
                first_scale,
                normed_one,
                query_pre,
                key_pre,
                gate_pre,
                query_rot,
                key_rot,
                values,
                query_scaled,
                key_scaled,
                weights,
                states,
                attended,
                out_scale,
                normed_out,
                mixed_heads,
                hidden,
                second_scale,
                (normed_two, normed_other),
                (own[0], other[0]),
                (own[1], other[1]),
                (own[2], other[2]),
            )
        )
        stream = hidden + glu_out
    mixed = low(stream)
    grad_stream = cotangent.astype(jnp.float32)
    collected = [None] * layer_count
    for layer_index in reversed(range(layer_count)):
        (
            stream_in,
            first_scale,
            normed_one,
            query_pre,
            key_pre,
            gate_pre,
            query_rot,
            key_rot,
            values,
            query_scaled,
            key_scaled,
            weights,
            states,
            attended,
            out_scale,
            normed_out,
            mixed_heads,
            hidden,
            second_scale,
            normed_pair,
            first_pair,
            second_pair,
            product_pair,
        ) = saved[layer_index]
        grad_low = low(grad_stream)
        grad_other = swap(grad_low, TP_BIT)

        def ffn_back(piece, number):
            product_grad = contract_cols(piece, w_third[layer_index])
            first_grad = low(product_grad * second_pair[number])
            second_grad = low(product_grad * first_pair[number])
            normed_grad = contract_cols(first_grad, w_first[layer_index]) + contract_cols(
                second_grad, w_second[layer_index]
            )
            return first_grad, second_grad, normed_grad

        other = ffn_back(grad_other, 1)
        own = ffn_back(grad_low, 0)
        normed_grad = own[2] + wide(swap(low(other[2]), TP_BIT))
        normed_both = chosen(jnp.concatenate(normed_pair), ffn_select)
        grad_both = chosen(jnp.concatenate([grad_low, grad_other]), ffn_select)
        ffn_parts = (
            reduce_weight(normed_both, jnp.concatenate([own[0], other[0]]), "none"),
            reduce_weight(normed_both, jnp.concatenate([own[1], other[1]]), "none"),
            reduce_weight(grad_both, jnp.concatenate(product_pair), "none"),
        )
        hidden_grad = grad_stream + rms_back(hidden, second_scale, normed_grad)
        branch_grad = low(hidden_grad)
        mixed_grad = contract_cols(branch_grad, w_out[layer_index])
        gate_grad = low(mixed_grad * normed_out)
        attended_grad = low(rms_back(attended, out_scale, mixed_grad * gate_pre))
        grads = attended_grad.reshape(length, heads, head_size)
        pulls = jnp.einsum("ihe,ihf->hef", query_scaled, grads, preferred_element_type=jnp.float32)
        carried = state_exchange(pulls, decay, doc_lengths, True)
        weight_grads = jnp.einsum("ihf,jhf->hij", grads, values, preferred_element_type=jnp.float32)
        score_grads = low(weight_grads * mask)
        rot_query_grad = jnp.einsum(
            "hij,jhe->ihe", score_grads, key_rot, preferred_element_type=jnp.float32
        ) + inward_wide * jnp.einsum("ihf,hef->ihe", grads, states, preferred_element_type=jnp.float32)
        rot_key_grad = jnp.einsum(
            "hij,ihe->jhe", score_grads, query_rot, preferred_element_type=jnp.float32
        ) + outward_wide * jnp.einsum("jhf,hef->jhe", values, carried, preferred_element_type=jnp.float32)
        value_grad = jnp.einsum(
            "hij,ihf->jhf", weights, grads, preferred_element_type=jnp.float32
        ) + jnp.einsum("jhe,hef->jhf", key_scaled, carried, preferred_element_type=jnp.float32)
        query_pre_grad = low(unrotate(rot_query_grad, cosine_table, sine_table) * swish_slope(query_pre))
        key_pre_grad = low(unrotate(rot_key_grad, cosine_table, sine_table) * swish_slope(key_pre))
        value_pre_grad = low(value_grad.reshape(length, model_width))
        last = layer_index == 0
        select = attention_select_last if last else attention_select
        tail = "tp_outer" if last else "outer_tp"
        normed_rows = chosen(normed_one, select)
        attention_parts = (
            reduce_weight(normed_rows, query_pre_grad, tail),
            reduce_weight(normed_rows, key_pre_grad, tail),
            reduce_weight(normed_rows, value_pre_grad, tail),
            reduce_weight(normed_rows, gate_grad, tail),
            reduce_weight(chosen(mixed_heads, select), branch_grad, tail),
        )
        normed_one_grad = (
            contract_cols(query_pre_grad, w_query[layer_index])
            + contract_cols(key_pre_grad, w_key[layer_index])
            + contract_cols(value_pre_grad, w_value[layer_index])
            + contract_cols(gate_grad, w_gate[layer_index])
        )
        grad_stream = hidden_grad + rms_back(stream_in, first_scale, normed_one_grad)
        collected[layer_index] = attention_parts + ffn_parts
    sums = [jnp.stack([collected[index][member] for index in range(layer_count)]) for member in range(8)]
    sums[7] = jnp.swapaxes(sums[7], 1, 2)
    return (mixed, grad_stream, *sums)


def solution(mesh):
    return jax.shard_map(
        local,
        mesh=mesh,
        in_specs=(
            P(("seq", "tp"), None),
            P(),
            P(),
            P(),
            P(),
            P(),
            P(None, None, "tp"),
            P(None, None, "tp"),
            P(None, "tp", None),
            P(),
            P(),
            P(("seq", "tp"), None),
        ),
        out_specs=(
            P(("seq", "tp"), None),
            P(("seq", "tp"), None),
            P(None, ("seq", "tp"), None),
            P(None, ("seq", "tp"), None),
            P(None, ("seq", "tp"), None),
            P(None, ("seq", "tp"), None),
            P(None, ("seq", "tp"), None),
            P(None, "seq", "tp"),
            P(None, "seq", "tp"),
            P(None, "tp", "seq"),
        ),
        check_vma=False,
    )
```
